32 devices in a mesh: grp: 2 (over x), chan: 16 (over z, y, core).
Axes of the slice: x: 2, y: 2, z: 4, core: 2. Of those that a mesh axis runs over, the one named last changes fastest.
Arguments:
- voltages: bfloat16 [2048, 38912], P(('grp', 'chan')), parts along dimension 0, may hold values from -6 to 6
- steering_delays: bfloat16 [512, 1024], replicated, may hold values from 0 to 1
- trial_delays: int32 [256, 512], replicated, may hold values from 0 to 7
- beam_order: int32 [512], replicated, may hold values from 0 to 511, each once
Outputs:
- trial_power: float32 [2, 1024, 4, 256], P(None, ('grp', 'chan')), parts along dimension 1
The draws below stay inside these ranges and needn't reach their ends.
There are 2 independent parts, one for each index of `grp`. The reference program is written for one: setup_inputs(seed, part) draws one part's arguments, and reference() takes and returns one part's arrays. A program takes and returns all parts, laid end to end along the dimension named above; an argument that names none is the same for every part. Nothing has to cross between parts.
Inputs may be any that keep to these rules, and one draw needn't show every extreme that they name: `beam_order`: each beam appears exactly once.
All inputs are finite; a program needn't handle non-finite values.
Results may differ from the reference program's by a relative error of at most 0.0094.
Values may be sent and summed in bfloat16 or wider, within the bound.
A program may use at most 64 MiB of HBM per device.

```python
import math
import jax
import jax.numpy as jnp
from jax import lax

TRANSFORM_SIZE = 2048
CHANNELS = 512
POLYPHASE_TAPS = 4
ANTENNAS = 1024
BEAM_COUNT = 512
TRIAL_COUNT = 256
BLOCK_FRAMES = 8
BLOCK_COUNT = 2
FLUCT_BINS = 4
ALL_FRAMES = 16
TOTAL_SAMPLES = 38912
N_CHAN = 16


def place_ends(drawn, stream_key, least, largest):
    spot = [jax.random.randint(jax.random.fold_in(stream_key, axis), (), 0, length) for axis, length in enumerate(drawn.shape)]
    longest = drawn.shape.index(max(drawn.shape))
    neighbour = spot[:longest] + [(spot[longest] + 1) % drawn.shape[longest]] + spot[longest + 1:]
    return drawn.at[tuple(spot)].set(least).at[tuple(neighbour)].set(largest)


def steps_of(stream_key, dims, pieces, least, largest):
    factor_of, own = 1.0, jax.random.fold_in(stream_key, 6)
    for dim, blocks in pieces:
        heights = jnp.exp(jax.random.uniform(jax.random.fold_in(own, dim), (blocks,), jnp.float32, least / len(pieces), largest / len(pieces)))
        factor_of = factor_of * jnp.repeat(heights, dims[dim] // blocks).reshape([-1 if axis == dim else 1 for axis in range(len(dims))])
    return factor_of


def noise(key, shape, width, most, split=(), held_as=jnp.bfloat16):
    entries = jax.random.normal(key, shape, jnp.float32) * width
    if len(split) > 0:
        entries = steps_of(key, shape, split, -0.22, 0.18) * entries
    return jnp.clip(entries, min=-most, max=most).astype(held_as)


def setup_inputs(seed: int = 0, part: int = 0) -> dict:
    arg_keys = jax.random.split(jax.random.key(seed), 5)
    own_keys = jax.random.split(jax.random.fold_in(arg_keys[4], part), 5)
    return {
        "voltages": noise(own_keys[0], (ANTENNAS, TOTAL_SAMPLES), 1.0, 6.0, ((0, 16),)),
        "steering_delays": jnp.clip(jax.random.uniform(arg_keys[1], (BEAM_COUNT, ANTENNAS), jnp.float32, 0.0, 1.0), 0.0, 1.0).astype(jnp.bfloat16),
        "trial_delays": place_ends(jax.random.randint(arg_keys[2], (TRIAL_COUNT, CHANNELS), 0, BLOCK_FRAMES), jax.random.fold_in(arg_keys[2], 1), 0, BLOCK_FRAMES - 1).astype(jnp.int32),
        "beam_order": jax.random.permutation(arg_keys[3], BEAM_COUNT).astype(jnp.int32),
    }


TWO_PI = 2.0 * math.pi

def prototype():
    length = POLYPHASE_TAPS * TRANSFORM_SIZE
    position = jnp.arange(length, dtype=jnp.float32)
    centred = (position - 0.5 * (length - 1)) / TRANSFORM_SIZE
    hamming = 0.54 - 0.46 * jnp.cos(TWO_PI * position / (length - 1))
    shaped = jnp.sinc(centred) * hamming
    return (shaped / jnp.sqrt(jnp.sum(shaped * shaped))).reshape(POLYPHASE_TAPS, TRANSFORM_SIZE)

def filter_table(channel_ids):
    sample = jnp.arange(TRANSFORM_SIZE, dtype=jnp.int32)
    phase_turns = channel_ids[:, None] * sample[None, :] % TRANSFORM_SIZE
    phase_angle = phase_turns.astype(jnp.float32) * (TWO_PI / TRANSFORM_SIZE)
    return jnp.concatenate([jnp.cos(phase_angle), -jnp.sin(phase_angle)], 0).astype(jnp.bfloat16)

def fluctuation_table():
    frame_index = jnp.arange(BLOCK_FRAMES, dtype=jnp.int32)
    bin_index = jnp.arange(1, FLUCT_BINS + 1, dtype=jnp.int32)
    phase_turns = frame_index[:, None] * bin_index[None, :] % BLOCK_FRAMES
    phase_angle = phase_turns.astype(jnp.float32) * (TWO_PI / BLOCK_FRAMES)
    return jnp.concatenate([jnp.cos(phase_angle), -jnp.sin(phase_angle)], 1).astype(jnp.bfloat16)

def trial_tables(trial_delays):
    bin_index = jnp.arange(1, FLUCT_BINS + 1, dtype=jnp.int32)
    phase_turns = bin_index[:, None, None] * trial_delays[None, :, :] % BLOCK_FRAMES
    phase_angle = phase_turns.astype(jnp.float32) * (TWO_PI / BLOCK_FRAMES)
    return (jnp.cos(phase_angle).astype(jnp.bfloat16), jnp.sin(phase_angle).astype(jnp.bfloat16))

def reference(voltages, steering_delays, trial_delays, beam_order):
    window = prototype()
    channel_ids = jnp.arange(CHANNELS, dtype=jnp.int32)
    table_float = filter_table(channel_ids).astype(jnp.float32).T
    grouped = voltages.reshape(N_CHAN, ANTENNAS // N_CHAN, ALL_FRAMES + POLYPHASE_TAPS - 1, TRANSFORM_SIZE)

    def filter_group(antenna_group):
        window_applied = antenna_group[:, 0:ALL_FRAMES, :].astype(jnp.float32) * window[0]
        for tap_index in range(1, POLYPHASE_TAPS):
            window_applied = window_applied + antenna_group[:, tap_index:tap_index + ALL_FRAMES, :].astype(jnp.float32) * window[tap_index]
        frame_rows = lax.optimization_barrier(window_applied.astype(jnp.bfloat16)).astype(jnp.float32).reshape(-1, TRANSFORM_SIZE)
        return jnp.dot(frame_rows, table_float, preferred_element_type=jnp.float32).astype(jnp.bfloat16)
    spectra = lax.map(filter_group, grouped)
    spectra = spectra.reshape(ANTENNAS, ALL_FRAMES, 2, CHANNELS).transpose(3, 2, 0, 1)
    steering = steering_delays.astype(jnp.float32)
    time_float = fluctuation_table().astype(jnp.float32)

    def beam_channel(inputs):
        channel, block_data = inputs
        factor = TWO_PI * (1.0 + channel / CHANNELS)
        phases = steering * factor
        cosine_weights = lax.optimization_barrier(jnp.cos(phases).astype(jnp.bfloat16)).astype(jnp.float32)
        sine_weights = lax.optimization_barrier(jnp.sin(phases).astype(jnp.bfloat16)).astype(jnp.float32)
        real_input = block_data[0].astype(jnp.float32).T
        imaginary_input = block_data[1].astype(jnp.float32).T
        beam_real = jnp.dot(real_input, cosine_weights.T, preferred_element_type=jnp.float32) + jnp.dot(imaginary_input, sine_weights.T, preferred_element_type=jnp.float32)
        beam_imag = jnp.dot(imaginary_input, cosine_weights.T, preferred_element_type=jnp.float32) - jnp.dot(real_input, sine_weights.T, preferred_element_type=jnp.float32)
        intensity = lax.optimization_barrier((beam_real * beam_real + beam_imag * beam_imag).astype(jnp.bfloat16))
        series = intensity.astype(jnp.float32).reshape(BLOCK_COUNT, BLOCK_FRAMES, BEAM_COUNT)
        return jnp.einsum('nfb,fj->njb', series, time_float).astype(jnp.bfloat16)
    fluctuation = lax.map(beam_channel, (jnp.arange(CHANNELS, dtype=jnp.float32), spectra))
    trial_cos, trial_sin = trial_tables(trial_delays)
    trial_cos = trial_cos.astype(jnp.float32)
    trial_sin = trial_sin.astype(jnp.float32)
    real_part = fluctuation[:, :, :FLUCT_BINS, :].astype(jnp.float32)
    imag_part = fluctuation[:, :, FLUCT_BINS:, :].astype(jnp.float32)
    sum_real = jnp.einsum('cnkb,kdc->nbkd', real_part, trial_cos) - jnp.einsum('cnkb,kdc->nbkd', imag_part, trial_sin)
    sum_imag = jnp.einsum('cnkb,kdc->nbkd', real_part, trial_sin) + jnp.einsum('cnkb,kdc->nbkd', imag_part, trial_cos)
    normaliser = 1.0 / (CHANNELS * BLOCK_FRAMES * ANTENNAS * ANTENNAS)
    power_all = (sum_real * sum_real + sum_imag * sum_imag) * normaliser
    return power_all[:, beam_order]
```

```python
import functools
import math

import jax
import jax.numpy as jnp
from jax import lax
from jax.experimental import pallas as pl
from jax.experimental.pallas import tpu as pltpu
from jax.sharding import PartitionSpec as P

TRANSFORM_SIZE = 2048
POLYPHASE_TAPS = 4
BLOCK_FRAMES = 8
FLUCT_BINS = 4

TWO_PI = 2.0 * math.pi
HALF_ROOT = math.sqrt(0.5)
ROWS = 16
COLS = 256


def prototype():
    length = POLYPHASE_TAPS * TRANSFORM_SIZE
    position = jnp.arange(length, dtype=jnp.float32)
    centred = (position - 0.5 * (length - 1)) / TRANSFORM_SIZE
    hamming = 0.54 - 0.46 * jnp.cos(TWO_PI * position / (length - 1))
    shaped = jnp.sinc(centred) * hamming
    return (shaped / jnp.sqrt(jnp.sum(shaped * shaped))).reshape(POLYPHASE_TAPS, TRANSFORM_SIZE)


def time_table(blocks):
    frame_index = jnp.arange(BLOCK_FRAMES, dtype=jnp.int32)
    bin_index = jnp.arange(1, FLUCT_BINS + 1, dtype=jnp.int32)
    turns = bin_index[:, None] * frame_index[None, :] % BLOCK_FRAMES
    angle = turns.astype(jnp.float32) * (TWO_PI / BLOCK_FRAMES)
    one = jnp.concatenate([jnp.cos(angle), -jnp.sin(angle)], 0)
    return jnp.kron(jnp.eye(blocks, dtype=jnp.float32), one).astype(jnp.bfloat16)


def eighth_cos(turns):
    folded = jnp.where(turns > 4, 8 - turns, turns)
    upper = jnp.where(folded == 0, 1.0, jnp.where(folded == 1, HALF_ROOT, 0.0))
    lower = jnp.where(folded == 4, -1.0, jnp.where(folded == 3, -HALF_ROOT, 0.0))
    return upper + lower


def trial_tables(trial_delays):
    bin_index = jnp.arange(1, FLUCT_BINS + 1, dtype=jnp.int32)
    turns = (bin_index[:, None, None] * trial_delays[None, :, :]) & (BLOCK_FRAMES - 1)
    cosine = eighth_cos(turns).astype(jnp.bfloat16)
    sine = eighth_cos((turns + 6) & (BLOCK_FRAMES - 1)).astype(jnp.bfloat16)
    return cosine, sine


def polynomial(x, coefficients):
    total = coefficients[-1]
    for value in coefficients[-2::-1]:
        total = total * x + value
    return total


COS_TERMS = [(-1.0) ** i / math.factorial(2 * i) for i in range(7)]
SIN_TERMS = [(-1.0) ** i / math.factorial(2 * i + 1) for i in range(7)]


def cos_sin_turns(turns):
    reduced = turns - jnp.floor(turns + 0.5)
    half = reduced * math.pi
    square = half * half
    cosine = polynomial(square, COS_TERMS)
    sine = half * polynomial(square, SIN_TERMS)
    return 1.0 - 2.0 * sine * sine, 2.0 * sine * cosine


def beam_kernel(channels, first_ref, steer_ref, x_ref, table_ref, out_ref, weights):
    group = x_ref.shape[0]
    frames = x_ref.shape[1] // 2
    antennas, beams = steer_ref.shape
    first = first_ref[0] + pl.program_id(0) * group
    factor = 1.0 + first.astype(jnp.float32) * (1.0 / channels)

    def rows_step(index, carry):
        rows = pl.ds(pl.multiple_of(index * ROWS, ROWS), ROWS)
        for start in range(0, beams, COLS):
            cols = pl.ds(start, COLS)
            delay = steer_ref[rows, cols].astype(jnp.float32)
            cosine, sine = cos_sin_turns(delay * factor)
            step = delay * (TWO_PI / channels)
            square = step * step
            step_cos = polynomial(square, COS_TERMS[:4])
            step_sin = step * polynomial(square, SIN_TERMS[:4])
            double = step_cos + step_cos
            cos_before = cosine * step_cos + sine * step_sin
            sin_before = sine * step_cos - cosine * step_sin
            for slot in range(group):
                weights[slot, 0, rows, cols] = cosine.astype(jnp.bfloat16)
                weights[slot, 1, rows, cols] = sine.astype(jnp.bfloat16)
                if slot + 1 < group:
                    cosine, cos_before = double * cosine - cos_before, cosine
                    sine, sin_before = double * sine - sin_before, sine
        return carry

    lax.fori_loop(0, antennas // ROWS, rows_step, 0)

    def channel_step(slot, carry):
        x = x_ref[slot]
        by_cos = jnp.dot(x, weights[slot, 0], preferred_element_type=jnp.float32)
        by_sin = jnp.dot(x, weights[slot, 1], preferred_element_type=jnp.float32)
        real = by_cos[:frames] + by_sin[frames:]
        imag = by_cos[frames:] - by_sin[:frames]
        intensity = (real * real + imag * imag).astype(jnp.bfloat16)
        out_ref[slot] = jnp.dot(
            table_ref[...], intensity, preferred_element_type=jnp.float32
        ).astype(jnp.bfloat16)
        return carry

    lax.fori_loop(0, group, channel_step, 0)


def form_beams(first, steering, spectra, table, channels):
    chan_local, double_frames, antennas = spectra.shape
    beams = steering.shape[1]
    group = math.gcd(chan_local, 8)
    rows = table.shape[0]
    return pl.pallas_call(
        functools.partial(beam_kernel, channels),
        grid=(chan_local // group,),
        out_shape=jax.ShapeDtypeStruct((chan_local, rows, beams), jnp.bfloat16),
        in_specs=[
            pl.BlockSpec(memory_space=pltpu.SMEM),
            pl.BlockSpec((antennas, beams), lambda i: (0, 0)),
            pl.BlockSpec((group, double_frames, antennas), lambda i: (i, 0, 0)),
            pl.BlockSpec(table.shape, lambda i: (0, 0)),
        ],
        out_specs=pl.BlockSpec((group, rows, beams), lambda i: (i, 0, 0)),
        scratch_shapes=[pltpu.VMEM((group, 2, antennas, beams), jnp.bfloat16)],
        compiler_params=pltpu.CompilerParams(vmem_limit_bytes=40 * 1024 * 1024),
    )(first, steering, spectra, table)


def shards(voltages, steering_delays, trial_delays, beam_order):
    devices = lax.axis_size("chan")
    device = lax.axis_index("chan")
    antenna_local, samples = voltages.shape
    beams, antennas = steering_delays.shape
    trials, channels = trial_delays.shape
    all_frames = samples // TRANSFORM_SIZE - POLYPHASE_TAPS + 1
    blocks = all_frames // BLOCK_FRAMES
    chan_local = channels // devices
    beam_local = beams // devices

    window = prototype()
    pieces = [
        voltages[:, i * TRANSFORM_SIZE : (i + 1) * TRANSFORM_SIZE]
        for i in range(all_frames + POLYPHASE_TAPS - 1)
    ]
    stacked = jnp.stack(pieces, 0)
    frames = stacked[:all_frames] * window[0]
    for tap in range(1, POLYPHASE_TAPS):
        frames = frames + stacked[tap : tap + all_frames] * window[tap]
    frame_rows = frames.astype(jnp.bfloat16).reshape(all_frames * antenna_local, TRANSFORM_SIZE)

    channel_ids = jnp.arange(channels, dtype=jnp.int32)
    sample = jnp.arange(TRANSFORM_SIZE, dtype=jnp.int32)
    turns = channel_ids[:, None] * sample[None, :] & (TRANSFORM_SIZE - 1)
    phase_turns = turns.astype(jnp.float32) * (1.0 / TRANSFORM_SIZE)
    cosine, sine = cos_sin_turns(phase_turns)
    filter_rows = jnp.stack([cosine.astype(jnp.bfloat16), (-sine).astype(jnp.bfloat16)], 0)
    filter_rows = filter_rows.reshape(2 * channels, TRANSFORM_SIZE)
    spectra = lax.dot_general(
        filter_rows, frame_rows, (((1,), (1,)), ((), ())), preferred_element_type=jnp.float32
    ).astype(jnp.bfloat16)
    spectra = spectra.reshape(2, devices, chan_local, all_frames * antenna_local)
    turned = lax.all_to_all(spectra, "chan", split_axis=1, concat_axis=1, tiled=True)
    turned = turned.reshape(2, devices, chan_local, all_frames, antenna_local)
    turned = turned.transpose(2, 0, 3, 1, 4).reshape(chan_local, 2 * all_frames, antennas)

    steering = steering_delays[beam_order].T
    first = (device * chan_local).astype(jnp.int32).reshape(1)
    fluctuation = form_beams(first, steering, turned, time_table(blocks), channels)

    outgoing = fluctuation.reshape(chan_local, 2 * FLUCT_BINS * blocks, devices, beam_local)
    outgoing = outgoing.transpose(2, 1, 3, 0)
    exchanged = lax.all_to_all(outgoing, "chan", split_axis=0, concat_axis=0, tiled=True)
    exchanged = exchanged.reshape(devices, blocks, 2, FLUCT_BINS, beam_local, chan_local)
    parts = exchanged.transpose(3, 1, 4, 2, 0, 5).reshape(
        FLUCT_BINS, blocks * beam_local, 2 * channels
    )
    trial_cos, trial_sin = trial_tables(trial_delays)
    both = jnp.concatenate(
        [
            jnp.concatenate([trial_cos, -trial_sin], 2),
            jnp.concatenate([trial_sin, trial_cos], 2),
        ],
        1,
    )
    sums = lax.dot_general(
        parts, both, (((2,), (2,)), ((0,), (0,))), preferred_element_type=jnp.float32
    )
    normaliser = 1.0 / (channels * BLOCK_FRAMES * antennas * antennas)
    sum_real, sum_imag = sums[..., :trials], sums[..., trials:]
    power = (sum_real * sum_real + sum_imag * sum_imag) * normaliser
    return power.reshape(FLUCT_BINS, blocks, beam_local, trials).transpose(1, 2, 0, 3)


def solution(mesh):
    return jax.shard_map(
        shards,
        mesh=mesh,
        in_specs=(P(("grp", "chan"), None), P(), P(), P()),
        out_specs=P(None, ("grp", "chan"), None, None),
        check_vma=False,
    )
```

```python
import functools
import math

import jax
import jax.numpy as jnp
from jax import lax
from jax.experimental import pallas as pl
from jax.experimental.pallas import tpu as pltpu
from jax.sharding import PartitionSpec as P

TRANSFORM_SIZE = 2048
POLYPHASE_TAPS = 4
BLOCK_FRAMES = 8
FLUCT_BINS = 4

TWO_PI = 2.0 * math.pi
HALF_ROOT = math.sqrt(0.5)
ROWS = 16
COLS = 256
LANES = 128


def prototype():
    length = POLYPHASE_TAPS * TRANSFORM_SIZE
    position = jnp.arange(length, dtype=jnp.float32)
    centred = (position - 0.5 * (length - 1)) / TRANSFORM_SIZE
    hamming = 0.54 - 0.46 * jnp.cos(TWO_PI * position / (length - 1))
    shaped = jnp.sinc(centred) * hamming
    return (shaped / jnp.sqrt(jnp.sum(shaped * shaped))).reshape(POLYPHASE_TAPS, TRANSFORM_SIZE)


def time_table(blocks):
    frame_index = jnp.arange(BLOCK_FRAMES, dtype=jnp.int32)
    bin_index = jnp.arange(1, FLUCT_BINS + 1, dtype=jnp.int32)
    turns = bin_index[:, None] * frame_index[None, :] % BLOCK_FRAMES
    angle = turns.astype(jnp.float32) * (TWO_PI / BLOCK_FRAMES)
    one = jnp.concatenate([jnp.cos(angle), -jnp.sin(angle)], 0)
    return jnp.kron(jnp.eye(blocks, dtype=jnp.float32), one).astype(jnp.bfloat16)


def eighth_cos(turns):
    folded = jnp.where(turns > 4, 8 - turns, turns)
    upper = jnp.where(folded == 0, 1.0, jnp.where(folded == 1, HALF_ROOT, 0.0))
    lower = jnp.where(folded == 4, -1.0, jnp.where(folded == 3, -HALF_ROOT, 0.0))
    return upper + lower


def trial_tables(trial_delays):
    bin_index = jnp.arange(1, FLUCT_BINS + 1, dtype=jnp.int32)
    turns = (bin_index[:, None, None] * trial_delays[None, :, :]) & (BLOCK_FRAMES - 1)
    cosine = eighth_cos(turns).astype(jnp.bfloat16)
    sine = eighth_cos((turns + 6) & (BLOCK_FRAMES - 1)).astype(jnp.bfloat16)
    return cosine, sine


def polynomial(x, coefficients):
    total = coefficients[-1]
    for value in coefficients[-2::-1]:
        total = total * x + value
    return total


COS_TERMS = [(-1.0) ** i / math.factorial(2 * i) for i in range(7)]
SIN_TERMS = [(-1.0) ** i / math.factorial(2 * i + 1) for i in range(7)]


def cos_sin_turns(turns):
    reduced = turns - jnp.floor(turns + 0.5)
    half = reduced * math.pi
    square = half * half
    cosine = polynomial(square, COS_TERMS)
    sine = half * polynomial(square, SIN_TERMS)
    return 1.0 - 2.0 * sine * sine, 2.0 * sine * cosine


def frame_kernel(window_ref, voltages_ref, out_ref):
    antenna_local, samples = voltages_ref.shape
    pieces = samples // TRANSFORM_SIZE

    def lane_step(index, carry):
        start = pl.multiple_of(index * LANES, LANES)
        window = [window_ref[tap, pl.ds(start, LANES)] for tap in range(POLYPHASE_TAPS)]
        for row in range(0, antenna_local, ROWS):
            held = []
            for piece in range(pieces):
                lanes = pl.ds(pl.multiple_of(start + piece * TRANSFORM_SIZE, LANES), LANES)
                held.append(voltages_ref[row : row + ROWS, lanes].astype(jnp.float32))
                if len(held) == POLYPHASE_TAPS:
                    total = held[0] * window[0]
                    for tap in range(1, POLYPHASE_TAPS):
                        total = total + held[tap] * window[tap]
                    frame = piece - POLYPHASE_TAPS + 1
                    first = frame * antenna_local + row
                    out_ref[first : first + ROWS, pl.ds(start, LANES)] = total.astype(jnp.bfloat16)
                    held = held[1:]
        return carry

    lax.fori_loop(0, TRANSFORM_SIZE // LANES, lane_step, 0)


def make_frames(window, voltages):
    antenna_local, samples = voltages.shape
    frames = samples // TRANSFORM_SIZE - POLYPHASE_TAPS + 1
    return pl.pallas_call(
        frame_kernel,
        out_shape=jax.ShapeDtypeStruct((frames * antenna_local, TRANSFORM_SIZE), jnp.bfloat16),
        in_specs=[pl.BlockSpec(memory_space=pltpu.VMEM)] * 2,
        out_specs=pl.BlockSpec(memory_space=pltpu.VMEM),
        compiler_params=pltpu.CompilerParams(vmem_limit_bytes=40 * 1024 * 1024),
    )(window, voltages)


def beam_kernel(
    channels, group, frames, first_ref, steer_ref, x_ref, table_ref, out_ref, weights, held
):
    antennas, beams = steer_ref.shape
    sources, rows_of_source, _ = x_ref.shape
    antenna_local = antennas // sources

    @pl.when(pl.program_id(0) == 0)
    def _():
        width = min(LANES, antenna_local)
        per = LANES // width
        block = lax.broadcasted_iota(jnp.int32, (rows_of_source, LANES), 1) // width
        for tile in range(antennas // LANES):
            for lane in range(0, frames * antenna_local, LANES * max(1, antenna_local // LANES)):
                if per == 1:
                    source = tile * LANES // antenna_local
                    offset = lane + tile * LANES % antenna_local
                    value = x_ref[source, :, offset : offset + LANES].astype(jnp.float32)
                    held[tile, pl.ds(lane // antenna_local, rows_of_source, stride=frames), :] = value
                    continue
                values = [
                    x_ref[tile * per + i, :, lane : lane + LANES].astype(jnp.float32)
                    for i in range(per)
                ]
                for j in range(per):
                    total = None
                    for i in range(per):
                        shift = (i - j) * width % LANES
                        value = pltpu.roll(values[i], shift, 1) if shift else values[i]
                        total = value if total is None else jnp.where(block == i, value, total)
                    frame = lane // LANES * per + j
                    held[tile, pl.ds(frame, rows_of_source, stride=frames), :] = total

    first = first_ref[0] + pl.program_id(0) * group
    factor = 1.0 + first.astype(jnp.float32) * (1.0 / channels)

    def rows_step(index, carry):
        rows = pl.ds(pl.multiple_of(index * ROWS, ROWS), ROWS)
        for start in range(0, beams, COLS):
            cols = pl.ds(start, COLS)
            delay = steer_ref[rows, cols].astype(jnp.float32)
            cosine, sine = cos_sin_turns(delay * factor)
            step = delay * (TWO_PI / channels)
            square = step * step
            step_cos = polynomial(square, COS_TERMS[:4])
            step_sin = step * polynomial(square, SIN_TERMS[:4])
            double = step_cos + step_cos
            cos_before = cosine * step_cos + sine * step_sin
            sin_before = sine * step_cos - cosine * step_sin
            for slot in range(group):
                weights[slot, 0, rows, cols] = cosine.astype(jnp.bfloat16)
                weights[slot, 1, rows, cols] = sine.astype(jnp.bfloat16)
                if slot + 1 < group:
                    cosine, cos_before = double * cosine - cos_before, cosine
                    sine, sin_before = double * sine - sin_before, sine
        return carry

    lax.fori_loop(0, antennas // ROWS, rows_step, 0)

    def channel_step(slot, carry):
        channel = pl.program_id(0) * group + slot
        spot = pl.ds(pl.multiple_of(channel * 2 * frames, 2 * frames), 2 * frames)
        x = jnp.concatenate([held[i, spot, :] for i in range(antennas // LANES)], 1)
        x = x.astype(jnp.bfloat16)
        by_cos = jnp.dot(x, weights[slot, 0], preferred_element_type=jnp.float32)
        by_sin = jnp.dot(x, weights[slot, 1], preferred_element_type=jnp.float32)
        real = by_cos[:frames] + by_sin[frames:]
        imag = by_cos[frames:] - by_sin[:frames]
        intensity = (real * real + imag * imag).astype(jnp.bfloat16)
        out_ref[slot] = jnp.dot(
            table_ref[...], intensity, preferred_element_type=jnp.float32
        ).astype(jnp.bfloat16)
        return carry

    lax.fori_loop(0, group, channel_step, 0)


def form_beams(first, steering, turned, table, channels, frames):
    sources, rows_of_source, _ = turned.shape
    chan_local = rows_of_source // 2
    antennas, beams = steering.shape
    group = math.gcd(chan_local, 8)
    rows = table.shape[0]
    return pl.pallas_call(
        functools.partial(beam_kernel, channels, group, frames),
        grid=(chan_local // group,),
        out_shape=jax.ShapeDtypeStruct((chan_local, rows, beams), jnp.bfloat16),
        in_specs=[
            pl.BlockSpec(memory_space=pltpu.SMEM),
            pl.BlockSpec((antennas, beams), lambda i: (0, 0)),
            pl.BlockSpec(turned.shape, lambda i: (0, 0, 0)),
            pl.BlockSpec(table.shape, lambda i: (0, 0)),
        ],
        out_specs=pl.BlockSpec((group, rows, beams), lambda i: (i, 0, 0)),
        scratch_shapes=[
            pltpu.VMEM((group, 2, antennas, beams), jnp.bfloat16),
            pltpu.VMEM((antennas // LANES, rows_of_source * frames, LANES), jnp.float32),
        ],
        compiler_params=pltpu.CompilerParams(vmem_limit_bytes=40 * 1024 * 1024),
    )(first, steering, turned, table)


def shards(voltages, steering_delays, trial_delays, beam_order):
    devices = lax.axis_size("chan")
    device = lax.axis_index("chan")
    antenna_local, samples = voltages.shape
    beams, antennas = steering_delays.shape
    trials, channels = trial_delays.shape
    all_frames = samples // TRANSFORM_SIZE - POLYPHASE_TAPS + 1
    blocks = all_frames // BLOCK_FRAMES
    chan_local = channels // devices
    beam_local = beams // devices

    frame_rows = make_frames(prototype(), voltages)
    row_ids = jnp.arange(2 * channels, dtype=jnp.int32)
    sample = jnp.arange(TRANSFORM_SIZE, dtype=jnp.int32)
    turns = (row_ids >> 1)[:, None] * sample[None, :] + ((row_ids & 1) * (TRANSFORM_SIZE // 4))[:, None]
    turns = ((turns + TRANSFORM_SIZE // 2) & (TRANSFORM_SIZE - 1)) - TRANSFORM_SIZE // 2
    half = turns.astype(jnp.float32) * (math.pi / TRANSFORM_SIZE)
    half_sine = half * polynomial(half * half, SIN_TERMS)
    filter_rows = (1.0 - 2.0 * half_sine * half_sine).astype(jnp.bfloat16)
    spectra = lax.dot_general(
        filter_rows, frame_rows, (((1,), (1,)), ((), ())), preferred_element_type=jnp.float32
    ).astype(jnp.bfloat16)
    spectra = spectra.reshape(devices, 2 * chan_local, all_frames * antenna_local)
    turned = lax.all_to_all(spectra, "chan", split_axis=0, concat_axis=0, tiled=True)

    steering = steering_delays[beam_order].T
    first = (device * chan_local).astype(jnp.int32).reshape(1)
    fluctuation = form_beams(first, steering, turned, time_table(blocks), channels, all_frames)

    outgoing = fluctuation.reshape(chan_local, 2 * FLUCT_BINS * blocks, devices, beam_local)
    outgoing = outgoing.transpose(2, 1, 3, 0)
    exchanged = lax.all_to_all(outgoing, "chan", split_axis=0, concat_axis=0, tiled=True)
    exchanged = exchanged.reshape(devices, blocks, 2, FLUCT_BINS, beam_local, chan_local)
    parts = exchanged.transpose(3, 1, 4, 2, 0, 5).reshape(
        FLUCT_BINS, blocks * beam_local, 2 * channels
    )
    trial_cos, trial_sin = trial_tables(trial_delays)
    both = jnp.concatenate(
        [
            jnp.concatenate([trial_cos, -trial_sin], 2),
            jnp.concatenate([trial_sin, trial_cos], 2),
        ],
        1,
    )
    sums = lax.dot_general(
        parts, both, (((2,), (2,)), ((0,), (0,))), preferred_element_type=jnp.float32
    )
    normaliser = 1.0 / (channels * BLOCK_FRAMES * antennas * antennas)
    sum_real, sum_imag = sums[..., :trials], sums[..., trials:]
    power = (sum_real * sum_real + sum_imag * sum_imag) * normaliser
    return power.reshape(FLUCT_BINS, blocks, beam_local, trials).transpose(1, 2, 0, 3)


def solution(mesh):
    return jax.shard_map(
        shards,
        mesh=mesh,
        in_specs=(P(("grp", "chan"), None), P(), P(), P()),
        out_specs=P(None, ("grp", "chan"), None, None),
        check_vma=False,
    )
```

```python
import functools
import math

import jax
import jax.numpy as jnp
from jax import lax
from jax.experimental import pallas as pl
from jax.experimental.pallas import tpu as pltpu
from jax.sharding import PartitionSpec as P

TRANSFORM_SIZE = 2048
POLYPHASE_TAPS = 4
BLOCK_FRAMES = 8
FLUCT_BINS = 4

TWO_PI = 2.0 * math.pi
HALF_ROOT = math.sqrt(0.5)
ROWS = 16
COLS = 256
LANES = 128


def prototype():
    length = POLYPHASE_TAPS * TRANSFORM_SIZE
    position = jnp.arange(length, dtype=jnp.float32)
    centred = (position - 0.5 * (length - 1)) / TRANSFORM_SIZE
    hamming = 0.54 - 0.46 * jnp.cos(TWO_PI * position / (length - 1))
    shaped = jnp.sinc(centred) * hamming
    return (shaped / jnp.sqrt(jnp.sum(shaped * shaped))).reshape(POLYPHASE_TAPS, TRANSFORM_SIZE)


def time_table(blocks):
    frame_index = jnp.arange(BLOCK_FRAMES, dtype=jnp.int32)
    bin_index = jnp.arange(1, FLUCT_BINS + 1, dtype=jnp.int32)
    turns = bin_index[:, None] * frame_index[None, :] % BLOCK_FRAMES
    angle = turns.astype(jnp.float32) * (TWO_PI / BLOCK_FRAMES)
    one = jnp.concatenate([jnp.cos(angle), -jnp.sin(angle)], 0)
    return jnp.kron(jnp.eye(blocks, dtype=jnp.float32), one).astype(jnp.bfloat16)


def eighth_cos(turns):
    folded = jnp.where(turns > 4, 8 - turns, turns)
    upper = jnp.where(folded == 0, 1.0, jnp.where(folded == 1, HALF_ROOT, 0.0))
    lower = jnp.where(folded == 4, -1.0, jnp.where(folded == 3, -HALF_ROOT, 0.0))
    return upper + lower


def trial_tables(trial_delays):
    bin_index = jnp.arange(1, FLUCT_BINS + 1, dtype=jnp.int32)
    turns = (bin_index[:, None, None] * trial_delays[None, :, :]) & (BLOCK_FRAMES - 1)
    cosine = eighth_cos(turns).astype(jnp.bfloat16)
    sine = eighth_cos((turns + 6) & (BLOCK_FRAMES - 1)).astype(jnp.bfloat16)
    return cosine, sine


def polynomial(x, coefficients):
    total = coefficients[-1]
    for value in coefficients[-2::-1]:
        total = total * x + value
    return total


COS_TERMS = [(-1.0) ** i / math.factorial(2 * i) for i in range(7)]
SIN_TERMS = [(-1.0) ** i / math.factorial(2 * i + 1) for i in range(7)]


def cos_sin_turns(turns):
    reduced = turns - jnp.floor(turns + 0.5)
    half = reduced * math.pi
    square = half * half
    cosine = polynomial(square, COS_TERMS)
    sine = half * polynomial(square, SIN_TERMS)
    return 1.0 - 2.0 * sine * sine, 2.0 * sine * cosine


def frame_kernel(window_ref, voltages_ref, out_ref):
    antenna_local, samples = voltages_ref.shape
    pieces = samples // TRANSFORM_SIZE

    def lane_step(index, carry):
        start = pl.multiple_of(index * LANES, LANES)
        window = [window_ref[tap, pl.ds(start, LANES)] for tap in range(POLYPHASE_TAPS)]
        for row in range(0, antenna_local, ROWS):
            held = []
            for piece in range(pieces):
                lanes = pl.ds(pl.multiple_of(start + piece * TRANSFORM_SIZE, LANES), LANES)
                held.append(voltages_ref[row : row + ROWS, lanes].astype(jnp.float32))
                if len(held) == POLYPHASE_TAPS:
                    total = held[0] * window[0]
                    for tap in range(1, POLYPHASE_TAPS):
                        total = total + held[tap] * window[tap]
                    frame = piece - POLYPHASE_TAPS + 1
                    first = frame * antenna_local + row
                    out_ref[first : first + ROWS, pl.ds(start, LANES)] = total.astype(jnp.bfloat16)
                    held = held[1:]
        return carry

    lax.fori_loop(0, TRANSFORM_SIZE // LANES, lane_step, 0)


def make_frames(window, voltages):
    antenna_local, samples = voltages.shape
    frames = samples // TRANSFORM_SIZE - POLYPHASE_TAPS + 1
    return pl.pallas_call(
        frame_kernel,
        out_shape=jax.ShapeDtypeStruct((frames * antenna_local, TRANSFORM_SIZE), jnp.bfloat16),
        in_specs=[pl.BlockSpec(memory_space=pltpu.VMEM)] * 2,
        out_specs=pl.BlockSpec(memory_space=pltpu.VMEM),
        compiler_params=pltpu.CompilerParams(vmem_limit_bytes=40 * 1024 * 1024),
    )(window, voltages)


def beam_kernel(
    channels, steer_ref, x_ref, table_ref, out_ref,
    weights, held, arrived, send_sem, recv_sem, own_sem,
):
    antennas, beams = steer_ref.shape
    sources, chunks, rows_of_chunk, width_of_source = x_ref.shape
    group = rows_of_chunk // 2
    antenna_local = antennas // sources
    frames = width_of_source // antenna_local
    me = lax.axis_index("chan")

    def greet(distance, carry):
        peer = lax.rem(me + distance, sources)
        pl.semaphore_signal(
            barrier, inc=1, device_id={"chan": peer}, device_id_type=pl.DeviceIdType.MESH
        )
        return carry

    barrier = pltpu.get_barrier_semaphore()
    lax.fori_loop(1, sources, greet, 0)
    pl.semaphore_wait(barrier, sources - 1)

    def to_peer(chunk, distance):
        peer = lax.rem(me + distance, sources)
        return pltpu.make_async_remote_copy(
            src_ref=x_ref.at[peer, chunk],
            dst_ref=arrived.at[chunk, me],
            send_sem=send_sem.at[chunk, distance - 1],
            recv_sem=recv_sem.at[chunk, distance - 1],
            device_id={"chan": peer},
            device_id_type=pl.DeviceIdType.MESH,
        )

    def own(chunk):
        return pltpu.make_async_copy(x_ref.at[me, chunk], arrived.at[chunk, me], own_sem.at[chunk])

    def send_chunk(chunk, carry):
        def send(distance, inner):
            to_peer(chunk, distance).start()
            return inner

        lax.fori_loop(1, sources, send, 0)
        own(chunk).start()
        return carry

    lax.fori_loop(0, chunks, send_chunk, 0)

    def arrange(chunk):
        width = min(LANES, antenna_local)
        per = LANES // width
        block = lax.broadcasted_iota(jnp.int32, (rows_of_chunk, LANES), 1) // width
        for tile in range(antennas // LANES):
            for lane in range(0, frames * antenna_local, LANES * max(1, antenna_local // LANES)):
                if per == 1:
                    source = tile * LANES // antenna_local
                    offset = lane + tile * LANES % antenna_local
                    value = arrived[chunk, source, :, offset : offset + LANES].astype(jnp.float32)
                    held[tile, pl.ds(lane // antenna_local, rows_of_chunk, stride=frames), :] = value
                    continue
                values = [
                    arrived[chunk, tile * per + i, :, lane : lane + LANES].astype(jnp.float32)
                    for i in range(per)
                ]
                for j in range(per):
                    total = None
                    for i in range(per):
                        shift = (i - j) * width % LANES
                        value = pltpu.roll(values[i], shift, 1) if shift else values[i]
                        total = value if total is None else jnp.where(block == i, value, total)
                    frame = lane // LANES * per + j
                    held[tile, pl.ds(frame, rows_of_chunk, stride=frames), :] = total

    def rows_step(factor, index):
        rows = pl.ds(pl.multiple_of(index * ROWS, ROWS), ROWS)
        for start in range(0, beams, COLS):
            cols = pl.ds(start, COLS)
            delay = steer_ref[rows, cols].astype(jnp.float32)
            cosine, sine = cos_sin_turns(delay * factor)
            step = delay * (TWO_PI / channels)
            square = step * step
            step_cos = polynomial(square, COS_TERMS[:4])
            step_sin = step * polynomial(square, SIN_TERMS[:4])
            double = step_cos + step_cos
            cos_before = cosine * step_cos + sine * step_sin
            sin_before = sine * step_cos - cosine * step_sin
            for slot in range(group):
                weights[slot, 0, rows, cols] = cosine.astype(jnp.bfloat16)
                weights[slot, 1, rows, cols] = sine.astype(jnp.bfloat16)
                if slot + 1 < group:
                    cosine, cos_before = double * cosine - cos_before, cosine
                    sine, sin_before = double * sine - sin_before, sine

    def channel_step(chunk, slot):
        spot = pl.ds(pl.multiple_of(slot * 2 * frames, 2 * frames), 2 * frames)
        x = jnp.concatenate([held[i, spot, :] for i in range(antennas // LANES)], 1)
        x = x.astype(jnp.bfloat16)
        by_cos = jnp.dot(x, weights[slot, 0], preferred_element_type=jnp.float32)
        by_sin = jnp.dot(x, weights[slot, 1], preferred_element_type=jnp.float32)
        real = by_cos[:frames] + by_sin[frames:]
        imag = by_cos[frames:] - by_sin[:frames]
        intensity = (real * real + imag * imag).astype(jnp.bfloat16)
        out_ref[chunk * group + slot] = jnp.dot(
            table_ref[...], intensity, preferred_element_type=jnp.float32
        ).astype(jnp.bfloat16)

    def chunk_step(chunk, carry):
        first = (me * chunks + chunk) * group
        factor = 1.0 + first.astype(jnp.float32) * (1.0 / channels)

        def rows_loop(index, inner):
            rows_step(factor, index)
            return inner

        def wait(distance, inner):
            to_peer(chunk, distance).wait_recv()
            return inner

        def channel_loop(slot, inner):
            channel_step(chunk, slot)
            return inner

        lax.fori_loop(0, antennas // ROWS, rows_loop, 0)
        lax.fori_loop(1, sources, wait, 0)
        own(chunk).wait()
        arrange(chunk)
        lax.fori_loop(0, group, channel_loop, 0)
        return carry

    lax.fori_loop(0, chunks, chunk_step, 0)

    def sent_chunk(chunk, carry):
        def sent(distance, inner):
            to_peer(chunk, distance).wait_send()
            return inner

        return lax.fori_loop(1, sources, sent, carry)

    lax.fori_loop(0, chunks, sent_chunk, 0)


def form_beams(steering, spectra, table, channels):
    sources, rows_of_source, width = spectra.shape
    chan_local = rows_of_source // 2
    antennas, beams = steering.shape
    frames = width * sources // antennas
    group = math.gcd(chan_local, 8)
    chunks = chan_local // group
    rows = table.shape[0]
    return pl.pallas_call(
        functools.partial(beam_kernel, channels),
        out_shape=jax.ShapeDtypeStruct((chan_local, rows, beams), jnp.bfloat16),
        in_specs=[pl.BlockSpec(memory_space=pltpu.VMEM)] * 3,
        out_specs=pl.BlockSpec(memory_space=pltpu.VMEM),
        scratch_shapes=[
            pltpu.VMEM((group, 2, antennas, beams), jnp.bfloat16),
            pltpu.VMEM((antennas // LANES, 2 * group * frames, LANES), jnp.float32),
            pltpu.VMEM((chunks, sources, 2 * group, width), jnp.bfloat16),
            pltpu.SemaphoreType.DMA((chunks, sources - 1)),
            pltpu.SemaphoreType.DMA((chunks, sources - 1)),
            pltpu.SemaphoreType.DMA((chunks,)),
        ],
        compiler_params=pltpu.CompilerParams(
            vmem_limit_bytes=40 * 1024 * 1024, collective_id=0, has_side_effects=True
        ),
    )(steering, spectra.reshape(sources, chunks, 2 * group, width), table)


def shards(voltages, steering_delays, trial_delays, beam_order):
    devices = lax.axis_size("chan")
    antenna_local, samples = voltages.shape
    beams, antennas = steering_delays.shape
    trials, channels = trial_delays.shape
    all_frames = samples // TRANSFORM_SIZE - POLYPHASE_TAPS + 1
    blocks = all_frames // BLOCK_FRAMES
    chan_local = channels // devices
    beam_local = beams // devices

    frame_rows = make_frames(prototype(), voltages)
    row_ids = jnp.arange(2 * channels, dtype=jnp.int32)
    sample = jnp.arange(TRANSFORM_SIZE, dtype=jnp.int32)
    turns = (row_ids >> 1)[:, None] * sample[None, :] + ((row_ids & 1) * (TRANSFORM_SIZE // 4))[:, None]
    turns = ((turns + TRANSFORM_SIZE // 2) & (TRANSFORM_SIZE - 1)) - TRANSFORM_SIZE // 2
    half = turns.astype(jnp.float32) * (math.pi / TRANSFORM_SIZE)
    half_sine = half * polynomial(half * half, SIN_TERMS)
    filter_rows = (1.0 - 2.0 * half_sine * half_sine).astype(jnp.bfloat16)
    spectra = lax.dot_general(
        filter_rows, frame_rows, (((1,), (1,)), ((), ())), preferred_element_type=jnp.float32
    ).astype(jnp.bfloat16)
    spectra = spectra.reshape(devices, 2 * chan_local, all_frames * antenna_local)
    steering = steering_delays[beam_order].T
    fluctuation = form_beams(steering, spectra, time_table(blocks), channels)

    outgoing = fluctuation.reshape(chan_local, 2 * FLUCT_BINS * blocks, devices, beam_local)
    outgoing = outgoing.transpose(2, 1, 3, 0)
    exchanged = lax.all_to_all(outgoing, "chan", split_axis=0, concat_axis=0, tiled=True)
    exchanged = exchanged.reshape(devices, blocks, 2, FLUCT_BINS, beam_local, chan_local)
    parts = exchanged.transpose(3, 1, 4, 2, 0, 5).reshape(
        FLUCT_BINS, blocks * beam_local, 2 * channels
    )
    trial_cos, trial_sin = trial_tables(trial_delays)
    both = jnp.concatenate(
        [
            jnp.concatenate([trial_cos, -trial_sin], 2),
            jnp.concatenate([trial_sin, trial_cos], 2),
        ],
        1,
    )
    sums = lax.dot_general(
        parts, both, (((2,), (2,)), ((0,), (0,))), preferred_element_type=jnp.float32
    )
    normaliser = 1.0 / (channels * BLOCK_FRAMES * antennas * antennas)
    sum_real, sum_imag = sums[..., :trials], sums[..., trials:]
    power = (sum_real * sum_real + sum_imag * sum_imag) * normaliser
    return power.reshape(FLUCT_BINS, blocks, beam_local, trials).transpose(1, 2, 0, 3)


def solution(mesh):
    return jax.shard_map(
        shards,
        mesh=mesh,
        in_specs=(P(("grp", "chan"), None), P(), P(), P()),
        out_specs=P(None, ("grp", "chan"), None, None),
        check_vma=False,
    )
```

```python
import functools
import math

import jax
import jax.numpy as jnp
from jax import lax
from jax.experimental import pallas as pl
from jax.experimental.pallas import tpu as pltpu
from jax.sharding import PartitionSpec as P

TRANSFORM_SIZE = 2048
POLYPHASE_TAPS = 4
BLOCK_FRAMES = 8
FLUCT_BINS = 4

TWO_PI = 2.0 * math.pi
HALF_ROOT = math.sqrt(0.5)
ROWS = 16
COLS = 256
LANES = 128


def prototype():
    length = POLYPHASE_TAPS * TRANSFORM_SIZE
    position = jnp.arange(length, dtype=jnp.float32)
    centred = (position - 0.5 * (length - 1)) / TRANSFORM_SIZE
    hamming = 0.54 - 0.46 * jnp.cos(TWO_PI * position / (length - 1))
    shaped = jnp.sinc(centred) * hamming
    return (shaped / jnp.sqrt(jnp.sum(shaped * shaped))).reshape(POLYPHASE_TAPS, TRANSFORM_SIZE)


def time_table(blocks):
    frame_index = jnp.arange(BLOCK_FRAMES, dtype=jnp.int32)
    bin_index = jnp.arange(1, FLUCT_BINS + 1, dtype=jnp.int32)
    turns = bin_index[:, None] * frame_index[None, :] % BLOCK_FRAMES
    angle = turns.astype(jnp.float32) * (TWO_PI / BLOCK_FRAMES)
    one = jnp.concatenate([jnp.cos(angle), -jnp.sin(angle)], 0)
    table = jnp.kron(jnp.eye(blocks, dtype=jnp.float32), one)
    table = table.reshape(blocks, 2, FLUCT_BINS, -1).transpose(2, 0, 1, 3)
    return table.reshape(2 * FLUCT_BINS * blocks, -1).astype(jnp.bfloat16)


def eighth_cos(turns):
    folded = jnp.where(turns > 4, 8 - turns, turns)
    upper = jnp.where(folded == 0, 1.0, jnp.where(folded == 1, HALF_ROOT, 0.0))
    lower = jnp.where(folded == 4, -1.0, jnp.where(folded == 3, -HALF_ROOT, 0.0))
    return upper + lower


def trial_tables(trial_delays):
    bin_index = jnp.arange(1, FLUCT_BINS + 1, dtype=jnp.int32)
    turns = (bin_index[:, None, None] * trial_delays[None, :, :]) & (BLOCK_FRAMES - 1)
    cosine = eighth_cos(turns).astype(jnp.bfloat16)
    sine = eighth_cos((turns + 6) & (BLOCK_FRAMES - 1)).astype(jnp.bfloat16)
    return cosine, sine


def polynomial(x, coefficients):
    total = coefficients[-1]
    for value in coefficients[-2::-1]:
        total = total * x + value
    return total


COS_TERMS = [(-1.0) ** i / math.factorial(2 * i) for i in range(7)]
SIN_TERMS = [(-1.0) ** i / math.factorial(2 * i + 1) for i in range(7)]


def cos_sin_turns(turns):
    reduced = turns - jnp.floor(turns + 0.5)
    half = reduced * math.pi
    square = half * half
    cosine = polynomial(square, COS_TERMS)
    sine = half * polynomial(square, SIN_TERMS)
    return 1.0 - 2.0 * sine * sine, 2.0 * sine * cosine


def frame_kernel(window_ref, voltages_ref, out_ref):
    antenna_local, samples = voltages_ref.shape
    pieces = samples // TRANSFORM_SIZE

    def lane_step(index, carry):
        start = pl.multiple_of(index * LANES, LANES)
        window = [window_ref[tap, pl.ds(start, LANES)] for tap in range(POLYPHASE_TAPS)]
        for row in range(0, antenna_local, ROWS):
            held = []
            for piece in range(pieces):
                lanes = pl.ds(pl.multiple_of(start + piece * TRANSFORM_SIZE, LANES), LANES)
                held.append(voltages_ref[row : row + ROWS, lanes].astype(jnp.float32))
                if len(held) == POLYPHASE_TAPS:
                    total = held[0] * window[0]
                    for tap in range(1, POLYPHASE_TAPS):
                        total = total + held[tap] * window[tap]
                    frame = piece - POLYPHASE_TAPS + 1
                    first = frame * antenna_local + row
                    out_ref[first : first + ROWS, pl.ds(start, LANES)] = total.astype(jnp.bfloat16)
                    held = held[1:]
        return carry

    lax.fori_loop(0, TRANSFORM_SIZE // LANES, lane_step, 0)


def make_frames(window, voltages):
    antenna_local, samples = voltages.shape
    frames = samples // TRANSFORM_SIZE - POLYPHASE_TAPS + 1
    return pl.pallas_call(
        frame_kernel,
        out_shape=jax.ShapeDtypeStruct((frames * antenna_local, TRANSFORM_SIZE), jnp.bfloat16),
        in_specs=[pl.BlockSpec(memory_space=pltpu.VMEM)] * 2,
        out_specs=pl.BlockSpec(memory_space=pltpu.VMEM),
        compiler_params=pltpu.CompilerParams(vmem_limit_bytes=40 * 1024 * 1024),
    )(window, voltages)


def beam_kernel(
    channels, steer_ref, x_ref, table_ref, out_ref,
    weights, held, arrived, send_sem, recv_sem, own_sem,
):
    antennas, beams = steer_ref.shape
    sources, chunks, rows_of_chunk, width_of_source = x_ref.shape
    group = rows_of_chunk // 2
    antenna_local = antennas // sources
    frames = width_of_source // antenna_local
    me = lax.axis_index("chan")

    def greet(distance, carry):
        peer = lax.rem(me + distance, sources)
        pl.semaphore_signal(
            barrier, inc=1, device_id={"chan": peer}, device_id_type=pl.DeviceIdType.MESH
        )
        return carry

    barrier = pltpu.get_barrier_semaphore()
    lax.fori_loop(1, sources, greet, 0)
    pl.semaphore_wait(barrier, sources - 1)

    def to_peer(chunk, distance):
        peer = lax.rem(me + distance, sources)
        return pltpu.make_async_remote_copy(
            src_ref=x_ref.at[peer, chunk],
            dst_ref=arrived.at[chunk, me],
            send_sem=send_sem.at[chunk, distance - 1],
            recv_sem=recv_sem.at[chunk, distance - 1],
            device_id={"chan": peer},
            device_id_type=pl.DeviceIdType.MESH,
        )

    def own(chunk):
        return pltpu.make_async_copy(x_ref.at[me, chunk], arrived.at[chunk, me], own_sem.at[chunk])

    def send_chunk(chunk, carry):
        def send(distance, inner):
            to_peer(chunk, distance).start()
            return inner

        lax.fori_loop(1, sources, send, 0)
        own(chunk).start()
        return carry

    lax.fori_loop(0, chunks, send_chunk, 0)

    def arrange(chunk):
        width = min(LANES, antenna_local)
        per = LANES // width
        block = lax.broadcasted_iota(jnp.int32, (rows_of_chunk, LANES), 1) // width
        for tile in range(antennas // LANES):
            for lane in range(0, frames * antenna_local, LANES * max(1, antenna_local // LANES)):
                if per == 1:
                    source = tile * LANES // antenna_local
                    offset = lane + tile * LANES % antenna_local
                    value = arrived[chunk, source, :, offset : offset + LANES].astype(jnp.float32)
                    held[tile, pl.ds(lane // antenna_local, rows_of_chunk, stride=frames), :] = value
                    continue
                values = [
                    arrived[chunk, tile * per + i, :, lane : lane + LANES].astype(jnp.float32)
                    for i in range(per)
                ]
                for j in range(per):
                    total = None
                    for i in range(per):
                        shift = (i - j) * width % LANES
                        value = pltpu.roll(values[i], shift, 1) if shift else values[i]
                        total = value if total is None else jnp.where(block == i, value, total)
                    frame = lane // LANES * per + j
                    held[tile, pl.ds(frame, rows_of_chunk, stride=frames), :] = total

    def rows_step(factor, index):
        rows = pl.ds(pl.multiple_of(index * ROWS, ROWS), ROWS)
        for start in range(0, beams, COLS):
            cols = pl.ds(start, COLS)
            delay = steer_ref[rows, cols].astype(jnp.float32)
            cosine, sine = cos_sin_turns(delay * factor)
            step = delay * (TWO_PI / channels)
            square = step * step
            step_cos = polynomial(square, COS_TERMS[:4])
            step_sin = step * polynomial(square, SIN_TERMS[:4])
            double = step_cos + step_cos
            cos_before = cosine * step_cos + sine * step_sin
            sin_before = sine * step_cos - cosine * step_sin
            for slot in range(group):
                weights[slot, 0, rows, cols] = cosine.astype(jnp.bfloat16)
                weights[slot, 1, rows, cols] = sine.astype(jnp.bfloat16)
                if slot + 1 < group:
                    cosine, cos_before = double * cosine - cos_before, cosine
                    sine, sin_before = double * sine - sin_before, sine

    def channel_step(chunk, slot):
        spot = pl.ds(pl.multiple_of(slot * 2 * frames, 2 * frames), 2 * frames)
        x = jnp.concatenate([held[i, spot, :] for i in range(antennas // LANES)], 1)
        x = x.astype(jnp.bfloat16)
        by_cos = jnp.dot(x, weights[slot, 0], preferred_element_type=jnp.float32)
        by_sin = jnp.dot(x, weights[slot, 1], preferred_element_type=jnp.float32)
        real = by_cos[:frames] + by_sin[frames:]
        imag = by_cos[frames:] - by_sin[:frames]
        intensity = (real * real + imag * imag).astype(jnp.bfloat16)
        out_ref[chunk * group + slot] = jnp.dot(
            table_ref[...], intensity, preferred_element_type=jnp.float32
        ).astype(jnp.bfloat16)

    def chunk_step(chunk, carry):
        first = (me * chunks + chunk) * group
        factor = 1.0 + first.astype(jnp.float32) * (1.0 / channels)

        def rows_loop(index, inner):
            rows_step(factor, index)
            return inner

        def wait(distance, inner):
            to_peer(chunk, distance).wait_recv()
            return inner

        def channel_loop(slot, inner):
            channel_step(chunk, slot)
            return inner

        lax.fori_loop(0, antennas // ROWS, rows_loop, 0)
        lax.fori_loop(1, sources, wait, 0)
        own(chunk).wait()
        arrange(chunk)
        lax.fori_loop(0, group, channel_loop, 0)
        return carry

    lax.fori_loop(0, chunks, chunk_step, 0)

    def sent_chunk(chunk, carry):
        def sent(distance, inner):
            to_peer(chunk, distance).wait_send()
            return inner

        return lax.fori_loop(1, sources, sent, carry)

    lax.fori_loop(0, chunks, sent_chunk, 0)


def form_beams(steering, spectra, table, channels):
    sources, rows_of_source, width = spectra.shape
    chan_local = rows_of_source // 2
    antennas, beams = steering.shape
    frames = width * sources // antennas
    group = math.gcd(chan_local, 8)
    chunks = chan_local // group
    rows = table.shape[0]
    return pl.pallas_call(
        functools.partial(beam_kernel, channels),
        out_shape=jax.ShapeDtypeStruct((chan_local, rows, beams), jnp.bfloat16),
        in_specs=[pl.BlockSpec(memory_space=pltpu.VMEM)] * 3,
        out_specs=pl.BlockSpec(memory_space=pltpu.VMEM),
        scratch_shapes=[
            pltpu.VMEM((group, 2, antennas, beams), jnp.bfloat16),
            pltpu.VMEM((antennas // LANES, 2 * group * frames, LANES), jnp.float32),
            pltpu.VMEM((chunks, sources, 2 * group, width), jnp.bfloat16),
            pltpu.SemaphoreType.DMA((chunks, sources - 1)),
            pltpu.SemaphoreType.DMA((chunks, sources - 1)),
            pltpu.SemaphoreType.DMA((chunks,)),
        ],
        compiler_params=pltpu.CompilerParams(
            vmem_limit_bytes=40 * 1024 * 1024, collective_id=0, has_side_effects=True
        ),
    )(steering, spectra.reshape(sources, chunks, 2 * group, width), table)


def shards(voltages, steering_delays, trial_delays, beam_order):
    devices = lax.axis_size("chan")
    antenna_local, samples = voltages.shape
    beams, antennas = steering_delays.shape
    trials, channels = trial_delays.shape
    all_frames = samples // TRANSFORM_SIZE - POLYPHASE_TAPS + 1
    blocks = all_frames // BLOCK_FRAMES
    chan_local = channels // devices
    beam_local = beams // devices

    frame_rows = make_frames(prototype(), voltages)
    row_ids = jnp.arange(2 * channels, dtype=jnp.int32)
    sample = jnp.arange(TRANSFORM_SIZE, dtype=jnp.int32)
    turns = (row_ids >> 1)[:, None] * sample[None, :] + ((row_ids & 1) * (TRANSFORM_SIZE // 4))[:, None]
    turns = ((turns + TRANSFORM_SIZE // 2) & (TRANSFORM_SIZE - 1)) - TRANSFORM_SIZE // 2
    half = turns.astype(jnp.float32) * (math.pi / TRANSFORM_SIZE)
    half_sine = half * polynomial(half * half, SIN_TERMS)
    filter_rows = (1.0 - 2.0 * half_sine * half_sine).astype(jnp.bfloat16)
    spectra = lax.dot_general(
        filter_rows, frame_rows, (((1,), (1,)), ((), ())), preferred_element_type=jnp.float32
    ).astype(jnp.bfloat16)
    spectra = spectra.reshape(devices, 2 * chan_local, all_frames * antenna_local)
    steering = steering_delays[beam_order].T
    fluctuation = form_beams(steering, spectra, time_table(blocks), channels)

    outgoing = fluctuation.reshape(chan_local, 2 * FLUCT_BINS * blocks, devices, beam_local)
    outgoing = outgoing.transpose(2, 1, 3, 0)
    exchanged = lax.all_to_all(outgoing, "chan", split_axis=0, concat_axis=0, tiled=True)
    parts = exchanged.reshape(devices, -1, chan_local).transpose(1, 0, 2)
    parts = parts.reshape(FLUCT_BINS, 2 * blocks * beam_local, channels)
    trial_cos, trial_sin = trial_tables(trial_delays)
    both = jnp.concatenate([trial_cos, trial_sin], 1)
    sums = lax.dot_general(
        parts, both, (((2,), (2,)), ((0,), (0,))), preferred_element_type=jnp.float32
    )
    normaliser = 1.0 / (channels * BLOCK_FRAMES * antennas * antennas)
    sums = sums.reshape(FLUCT_BINS, blocks, 2, beam_local, 2 * trials)
    real, imag = sums[:, :, 0], sums[:, :, 1]
    sum_real = real[..., :trials] - imag[..., trials:]
    sum_imag = real[..., trials:] + imag[..., :trials]
    power = (sum_real * sum_real + sum_imag * sum_imag) * normaliser
    return power.reshape(FLUCT_BINS, blocks, beam_local, trials).transpose(1, 2, 0, 3)


def solution(mesh):
    return jax.shard_map(
        shards,
        mesh=mesh,
        in_specs=(P(("grp", "chan"), None), P(), P(), P()),
        out_specs=P(None, ("grp", "chan"), None, None),
        check_vma=False,
    )
```
